32 devices in a mesh: groups: 2 (over y), tile: 4 (over z), tracer: 4 (over x, core).
Axes of the slice: x: 2, y: 2, z: 4, core: 2. Of those that a mesh axis runs over, the one named last changes fastest.
Arguments:
- species_amounts: float32 [64, 32, 128, 128], P(('groups', 'tracer'), None, 'tile'), parts along dimension 0, may hold values from 0.2 to 2
- face_currents: float32 [2, 64, 128, 128], P(None, 'groups', 'tile'), parts along dimension 1, may hold values from -1 to 1
- thermal_anomaly: float32 [64, 128, 128], P(('groups', 'tracer'), 'tile'), parts along dimension 0, may hold values from -4 to 4
- layer_total_per_profile: int32 [256, 128], P(('groups', 'tile')), parts along dimension 0, may hold values from 0 to 32
- consumed_species: int32 [32], replicated, may hold values from 0 to 31, each once
- attenuation_factor: float32 [32], replicated, may hold values from 0.009375 to 0.09375
- intake_speedup: float32 [32], replicated, may hold values from 0.3 to 3
- incoming_sunshine: float32 [256, 128], P(('groups', 'tile')), parts along dimension 0, may hold values from 0.5 to 2
Outputs:
- tracers_out: float32 [64, 32, 128, 128], P('groups', 'tracer', 'tile'), parts along dimension 0
- velocity_out: float32 [2, 64, 128, 128], P(None, ('groups', 'tracer'), 'tile'), parts along dimension 1
- temperature_out: float32 [64, 128, 128], P(('groups', 'tracer'), 'tile'), parts along dimension 0
The draws below stay inside these ranges and needn't reach their ends.
There are 2 independent parts, one for each index of `groups`. The reference program is written for one: setup_inputs(seed, part) draws one part's arguments, and reference() takes and returns one part's arrays. A program takes and returns all parts, laid end to end along the dimension named above; an argument that names none is the same for every part. Nothing has to cross between parts.
Inputs may be any that keep to these rules, and one draw needn't show every extreme that they name: Levels 0 to layer_total_per_profile - 1 of a column are sea, deeper levels are land; 0 marks a land column. `consumed_species`: A permutation of the 32 tracers.
All inputs are finite; a program needn't handle non-finite values.
Results may differ from the reference program's by a relative error of at most 0.0003.
Values sent between devices are 32-bit elements; how exact they have to be, the bound alone decides.
No kernel may reach another device: no remote copies, remote signals or barrier semaphores. Data moves between devices by JAX's collectives and lax.ppermute only.
A program may use at most 64 MiB of HBM per device.

```python
import math
import jax
import jax.numpy as jnp
from jax import lax

NTR = 32
DEPTH_LAYERS = 32
GRID_MERIDIONAL = 128
GRID_ZONAL = 128


def place_ends(entries, rng, smallest, largest):
    extent = entries.shape
    place = [jax.random.randint(jax.random.fold_in(rng, axis), (), 0, extent[axis]) for axis in range(len(extent))]
    entries = entries.at[tuple(place)].set(smallest)
    longest = extent.index(max(extent))
    place[longest] = (place[longest] + 1) % extent[longest]
    return entries.at[tuple(place)].set(largest)


def level_of(rng, shape, shards, least, largest):
    loudness = 1.0
    for axis_at, parts in shards:
        draws = jax.random.uniform(jax.random.fold_in(jax.random.fold_in(rng, 6), axis_at), (parts,), jnp.float32, least / len(shards), largest / len(shards))
        loudness = loudness * jnp.repeat(jnp.exp(draws), shape[axis_at] // parts).reshape((-1,) + (1,) * (len(shape) - 1 - axis_at))
    return loudness


def scatter_about(stream_key, dims, deviation, bound, pieces=(), held_as=jnp.bfloat16):
    loudness = level_of(stream_key, dims, pieces, -0.22, 0.18) if pieces else 1.0
    array = jax.random.normal(stream_key, dims, jnp.float32) * deviation * loudness
    return jnp.minimum(jnp.maximum(array, -bound), bound).astype(held_as)


def setup_inputs(seed: int = 0, part: int = 0) -> dict:
    key_list = jax.random.split(jax.random.key(seed), 9)
    part_splits = jax.random.split(jax.random.fold_in(key_list[8], part), 9)
    return {
        "species_amounts": jnp.clip(jnp.exp(math.log(2.0) - 2.3025851 * jax.random.uniform(part_splits[0], (NTR, DEPTH_LAYERS, GRID_ZONAL, GRID_MERIDIONAL), jnp.float32) ** level_of(part_splits[0], (NTR, DEPTH_LAYERS, GRID_ZONAL, GRID_MERIDIONAL), ((0, 4), (2, 4)), -0.2, 0.2)), 0.2, 2.0),
        "face_currents": jnp.clip(jax.random.uniform(part_splits[1], (2, DEPTH_LAYERS, GRID_ZONAL, GRID_MERIDIONAL), jnp.float32, -1.0, 1.0) * level_of(part_splits[1], (2, DEPTH_LAYERS, GRID_ZONAL, GRID_MERIDIONAL), ((2, 4),), -0.4, 0.0), -1.0, 1.0),
        "thermal_anomaly": scatter_about(part_splits[2], (DEPTH_LAYERS, GRID_ZONAL, GRID_MERIDIONAL), 1.0, 4.0, ((0, 4), (1, 4)), jnp.float32),
        "layer_total_per_profile": place_ends(jax.random.randint(part_splits[3], (GRID_ZONAL, GRID_MERIDIONAL), 0, DEPTH_LAYERS + 1), jax.random.fold_in(part_splits[3], 1), 0, DEPTH_LAYERS).astype(jnp.int32),
        "consumed_species": jax.random.permutation(key_list[4], NTR).astype(jnp.int32),
        "attenuation_factor": jnp.clip(jnp.exp(jax.random.uniform(key_list[5], (NTR,), jnp.float32, math.log(0.009375), math.log(0.09375))), 0.009375, 0.09375),
        "intake_speedup": jnp.clip(jnp.exp(jax.random.uniform(key_list[6], (NTR,), jnp.float32, math.log(0.3), math.log(3.0))), 0.3, 3.0),
        "incoming_sunshine": jnp.clip(jnp.exp(math.log(2.0) - 1.3862944 * jax.random.uniform(part_splits[7], (GRID_ZONAL, GRID_MERIDIONAL), jnp.float32) ** level_of(part_splits[7], (GRID_ZONAL, GRID_MERIDIONAL), ((0, 4),), -0.2, 0.2)), 0.5, 2.0),
    }


sub_step = 0.45
step_duration = 0.2
gravity = 0.5
viscosity = 0.2
coriolis_base = 0.5
beta_plane = 0.5
spreading_coefficient = 0.2
water_clear = 0.05
column_optical = 3.0
warming_coefficient = 5.0
light_half = 0.3
nutrient_half = 0.5


def wraparound_border(values, margin, along):
    length = values.shape[along]
    leading = lax.slice_in_dim(values, length - margin, length, axis=along)
    trailing = lax.slice_in_dim(values, 0, margin, axis=along)
    return jnp.concatenate([leading, values, trailing], axis=along)


def shift_south(values):
    return jnp.concatenate([jnp.zeros_like(values[..., :1]), values[..., :-1]], axis=-1)


def shift_north(values, offset=1):
    return jnp.concatenate([values[..., offset:], jnp.zeros_like(values[..., :offset])], axis=-1)


def wet_levels(depth_ext, first_level, level_count):
    levels = first_level + jnp.arange(level_count, dtype=jnp.int32)
    return (levels[:, None, None] < depth_ext[None]).astype(jnp.float32)


def limiter(left_slope, right_slope):
    smaller = jnp.minimum(jnp.abs(left_slope), jnp.abs(right_slope))
    return jnp.where(left_slope * right_slope > 0.0, jnp.sign(left_slope) * smaller, 0.0)


def face_flux(behind, centre, forward, beyond, speed):
    positive = speed * (centre + 0.5 * limiter(centre - behind, forward - centre))
    negative = speed * (forward - 0.5 * limiter(forward - centre, beyond - forward))
    return jnp.where(speed > 0.0, positive, negative)


def face_speeds(velocity_with_halo_border, wet_ext):
    east_speed = velocity_with_halo_border[0][:, :-1] * wet_ext[:, :-1] * wet_ext[:, 1:]
    north_speed = velocity_with_halo_border[1] * wet_ext * shift_north(wet_ext)
    return east_speed, north_speed


def flux_substep(extended, east_speed, north_speed):
    length = extended.shape[2]
    east_flux = face_flux(extended[:, :, 0:length - 3], extended[:, :, 1:length - 2],
                          extended[:, :, 2:length - 1], extended[:, :, 3:length],
                          east_speed[:, 1:length - 2])
    middle = extended[:, :, 2:length - 2]
    north_flux = face_flux(shift_south(middle), middle, shift_north(middle), shift_north(middle, 2),
                           north_speed[:, 2:length - 2])
    spread = (east_flux[:, :, 1:] - east_flux[:, :, :-1]) + (north_flux - shift_south(north_flux))
    return middle - sub_step * spread


def laplacian(values):
    inner = values[:, 1:-1]
    return values[:, 2:] + values[:, :-2] + shift_north(inner) + shift_south(inner) - 4.0 * inner


def velocity_advance(flow_one, marine_mask_profile, thermal_profile_alone):
    east_vel = flow_one[0]
    north_vel = flow_one[1]
    ocean_profiles = east_vel.shape[1] - 2
    coriolis_y = coriolis_base + beta_plane * jnp.arange(east_vel.shape[2], dtype=jnp.float32) / east_vel.shape[2]
    centre_u = east_vel[:, 1:ocean_profiles + 1]
    centre_v = north_vel[:, 1:ocean_profiles + 1]
    v_bar = 0.25 * (centre_v + north_vel[:, 2:] + shift_south(centre_v) + shift_south(north_vel[:, 2:]))
    u_bar = 0.25 * (centre_u + east_vel[:, :-2] + shift_north(centre_u) + shift_north(east_vel[:, :-2]))
    marine_mask_interior = marine_mask_profile[:, 1:ocean_profiles + 1]
    east_open = marine_mask_interior * marine_mask_profile[:, 2:]
    north_open = marine_mask_interior * shift_north(marine_mask_interior)
    heat_mid = thermal_profile_alone[:, 1:ocean_profiles + 1]
    new_east = east_open * (centre_u + step_duration * (coriolis_y * v_bar - gravity * (thermal_profile_alone[:, 2:] - heat_mid)
                                                    + viscosity * laplacian(east_vel)))
    new_north = north_open * (centre_v + step_duration * (-coriolis_y * u_bar - gravity * (shift_north(heat_mid) - heat_mid)
                                                      + viscosity * laplacian(north_vel)))
    return jnp.stack([new_east, new_north]), laplacian(thermal_profile_alone)


def optical_thickness(by_cells, attenuation_factor):
    summed = jnp.tensordot(attenuation_factor, jnp.abs(by_cells), axes=1, precision=lax.Precision.HIGHEST)
    return (water_clear + summed) * (column_optical / DEPTH_LAYERS)


def react(by_cells, optical, overhead, wet_mask, incoming_sunshine, intake_speedup, consumed_species):
    depth_tau = overhead[None] + (jnp.cumsum(optical, axis=0) - optical)
    reaching = incoming_sunshine[None] * jnp.exp(-depth_tau)
    absorbed_part = 1.0 - jnp.exp(-optical)
    captured_radiance = reaching * absorbed_part * wet_mask
    mean_light = reaching * absorbed_part / optical
    light_limit = mean_light / (mean_light + light_half)
    pairing = (consumed_species[:, None] == jnp.arange(by_cells.shape[0], dtype=jnp.int32)[None]).astype(jnp.float32)
    nutrient = jnp.tensordot(pairing, by_cells, axes=1, precision=lax.Precision.HIGHEST)
    uptake = intake_speedup[:, None, None, None] * light_limit[None] * by_cells * nutrient / (nutrient_half + jnp.abs(nutrient))
    consumed = jnp.tensordot(pairing.T, uptake, axes=1, precision=lax.Precision.HIGHEST)
    updated = by_cells + wet_mask[None] * (uptake - consumed)
    return updated, captured_radiance


def reference(species_amounts, face_currents, thermal_anomaly, layer_total_per_profile, consumed_species, attenuation_factor, intake_speedup, incoming_sunshine):
    wet_ext = wet_levels(wraparound_border(layer_total_per_profile, 2, 0), 0, DEPTH_LAYERS)
    velocity_with_halo_border = wraparound_border(face_currents, 2, 2)
    east_speed, north_speed = face_speeds(velocity_with_halo_border, wet_ext)

    def advect_one(single):
        values = single[None]
        for repeat in range(2):
            values = flux_substep(wraparound_border(values, 2, 2), east_speed, north_speed)
        return values[0]

    advected = lax.map(advect_one, species_amounts)
    marine_mask_profile = wet_ext[:, 1:-1]
    advanced_face_speeds, thermal_second_derivative = velocity_advance(velocity_with_halo_border[:, :, 1:-1], marine_mask_profile, wraparound_border(thermal_anomaly, 1, 1))
    marine_mask_interior = marine_mask_profile[:, 1:-1]
    optical = optical_thickness(advected, attenuation_factor)
    overhead = jnp.zeros(optical.shape[1:], jnp.float32)
    updated, captured_radiance = react(advected, optical, overhead, marine_mask_interior, incoming_sunshine, intake_speedup, consumed_species)
    advanced_thermal_field = marine_mask_interior * (thermal_anomaly + step_duration * spreading_coefficient * thermal_second_derivative + warming_coefficient * captured_radiance)
    return updated, advanced_face_speeds, advanced_thermal_field
```

```python
import functools

import jax
import jax.numpy as jnp
from jax import lax
from jax.experimental import pallas as pl
from jax.experimental.pallas import tpu as pltpu
from jax.sharding import PartitionSpec as P

sub_step = 0.45
step_duration = 0.2
gravity = 0.5
viscosity = 0.2
coriolis_base = 0.5
beta_plane = 0.5
spreading_coefficient = 0.2
water_clear = 0.05
column_optical = 3.0
warming_coefficient = 5.0
light_half = 0.3
nutrient_half = 0.5

SUB = 8
REACH = 4
EXTRA = 8


def shift_south(values):
    return jnp.concatenate([jnp.zeros_like(values[..., :1]), values[..., :-1]], axis=-1)


def shift_north(values, offset=1):
    return jnp.concatenate([values[..., offset:], jnp.zeros_like(values[..., :offset])], axis=-1)


def laplacian(values):
    inner = values[:, 1:-1]
    return values[:, 2:] + values[:, :-2] + shift_north(inner) + shift_south(inner) - 4.0 * inner


def velocity_advance(flow_one, marine_mask_profile, thermal_profile_alone):
    east_vel = flow_one[0]
    north_vel = flow_one[1]
    ocean_profiles = east_vel.shape[1] - 2
    coriolis_y = (
        coriolis_base
        + beta_plane * jnp.arange(east_vel.shape[2], dtype=jnp.float32) / east_vel.shape[2]
    )
    centre_u = east_vel[:, 1 : ocean_profiles + 1]
    centre_v = north_vel[:, 1 : ocean_profiles + 1]
    v_bar = 0.25 * (
        centre_v + north_vel[:, 2:] + shift_south(centre_v) + shift_south(north_vel[:, 2:])
    )
    u_bar = 0.25 * (
        centre_u + east_vel[:, :-2] + shift_north(centre_u) + shift_north(east_vel[:, :-2])
    )
    marine_mask_interior = marine_mask_profile[:, 1 : ocean_profiles + 1]
    east_open = marine_mask_interior * marine_mask_profile[:, 2:]
    north_open = marine_mask_interior * shift_north(marine_mask_interior)
    heat_mid = thermal_profile_alone[:, 1 : ocean_profiles + 1]
    new_east = east_open * (
        centre_u
        + step_duration
        * (
            coriolis_y * v_bar
            - gravity * (thermal_profile_alone[:, 2:] - heat_mid)
            + viscosity * laplacian(east_vel)
        )
    )
    new_north = north_open * (
        centre_v
        + step_duration
        * (
            -coriolis_y * u_bar
            - gravity * (shift_north(heat_mid) - heat_mid)
            + viscosity * laplacian(north_vel)
        )
    )
    return jnp.stack([new_east, new_north]), laplacian(thermal_profile_alone)


def pack_kernel(
    tracers, own_levels, c_low, c_high, uv_low, uv_high, heat, depth, to_next, to_previous
):
    rows = depth.shape[0]
    base = REACH * tracers
    for t in range(tracers):
        place = pl.ds(REACH * t, REACH)
        to_next[:, place, :] = c_high[t, :, SUB - REACH :, :]
        to_previous[:, place, :] = c_low[t, :, :REACH, :]
    to_next[:, base : base + 3, :] = uv_high[0, :, SUB - 3 :, :]
    to_next[:, base + 3 : base + 5, :] = uv_high[1, :, SUB - 2 :, :]
    to_previous[:, base : base + 3, :] = uv_low[0, :, :3, :]
    to_previous[:, base + 3 : base + 5, :] = uv_low[1, :, :2, :]

    @pl.when(pl.program_id(0) == 0)
    def _():
        for level in range(own_levels):
            to_next[level, base + 5 : base + 6, :] = heat[level, rows - 1 : rows, :]
            to_previous[level, base + 5 : base + 6, :] = heat[level, 0:1, :]
        for row in range(REACH):
            start = rows - REACH + row
            to_next[row, base + 6 : base + 7, :] = depth[start : start + 1, :].astype(jnp.float32)
            to_previous[row, base + 6 : base + 7, :] = depth[row : row + 1, :].astype(jnp.float32)


def pack(species, currents, heat, depth):
    tracers, levels, rows, width = species.shape
    height = REACH * tracers + EXTRA
    last = rows // SUB - 1
    out = jax.ShapeDtypeStruct((levels, height, width), jnp.float32)
    out_spec = pl.BlockSpec((SUB, height, width), lambda g: (g, 0, 0))
    return pl.pallas_call(
        functools.partial(pack_kernel, tracers, heat.shape[0]),
        grid=(levels // SUB,),
        in_specs=[
            pl.BlockSpec((tracers, SUB, SUB, width), lambda g: (0, g, 0, 0)),
            pl.BlockSpec((tracers, SUB, SUB, width), lambda g: (0, g, last, 0)),
            pl.BlockSpec((2, SUB, SUB, width), lambda g: (0, g, 0, 0)),
            pl.BlockSpec((2, SUB, SUB, width), lambda g: (0, g, last, 0)),
            pl.BlockSpec(heat.shape, lambda g: (0, 0, 0)),
            pl.BlockSpec(depth.shape, lambda g: (0, 0)),
        ],
        out_specs=[out_spec, out_spec],
        out_shape=[out, out],
        name="pack",
        cost_estimate=pl.CostEstimate(
            flops=0, transcendentals=0, bytes_accessed=levels * height * width * 4 * 4
        ),
    )(species, species, currents, currents, heat, depth)


class Rows:
    def __init__(self, cells, east, north, lanes):
        self.cells, self.east, self.north = cells, east, north
        self.first, self.last = lanes
        self.kept = {}

    def keep(self, name, row, make):
        key = (name, row)
        if key not in self.kept:
            self.kept[key] = make()
        return self.kept[key]

    def half(self, row):
        return self.keep("half", row, lambda: 0.5 * self.cells(row))

    def slope(self, row):
        return self.keep("slope", row, lambda: self.half(row + 1) - self.half(row))

    def edges(self, row):
        def make():
            limited = limit(self.slope(row - 1), self.slope(row))
            return self.cells(row) + limited, self.cells(row) - limited

        return self.keep("edges", row, make)

    def east_flux(self, row):
        def make():
            speed = self.east(row)
            return speed * jnp.where(speed > 0.0, self.edges(row)[0], self.edges(row + 1)[1])

        return self.keep("flux", row, make)

    def north_spread(self, row):
        width = self.half(row).shape[1]
        half = self.half(row)
        slope = jnp.where(self.last, 0.0, pltpu.roll(half, width - 1, 1)) - half
        before = jnp.where(self.first, half, pltpu.roll(slope, 1, 1))
        limited = limit(before, slope)
        speed = self.north(row)
        cell = self.cells(row)
        ahead = pltpu.roll(cell - limited, width - 1, 1)
        flux = speed * jnp.where(speed > 0.0, cell + limited, ahead)
        return flux - pltpu.roll(flux, 1, 1)

    def new(self, row):
        def make():
            spread = (self.east_flux(row) - self.east_flux(row - 1)) + self.north_spread(row)
            return self.cells(row) - spread

        return self.keep("new", row, make)


def limit(one, other):
    low = jnp.minimum(one, other)
    high = jnp.maximum(one, other)
    return jnp.maximum(low, jnp.minimum(high, 0.0))


def advect_kernel(
    plan, me_ref, attenuation, c_ref, uv_ref, depth_ref, *refs
):
    rows, levels, tracers_here, first, count, own, low, high, width = (
        plan["rows"],
        plan["levels"],
        plan["tracers"],
        plan["first"],
        plan["count"],
        plan["own_levels"],
        plan["low"],
        plan["high"],
        plan["width"],
    )
    devices = levels // own
    shared, pieces = max(1, SUB // own), max(1, own // SUB)
    tall = high - low
    main = own * count * tall
    if plan["halo"]:
        halo_ref, halo_top = refs[:2]
        refs = refs[2:]
    outs = refs[:devices]
    buffer, east, north, shade, sums, sems = refs[devices:]
    height = REACH * tracers_here + EXTRA
    base = REACH * tracers_here
    me = me_ref[0]
    step = pl.program_id(0)
    if shared > 1:
        group = lax.bitwise_xor(me // shared, step)
    else:
        group = lax.bitwise_xor(me, step // pieces) * pieces + lax.rem(step, pieces)

    lane = lax.broadcasted_iota(jnp.int32, (SUB, width), 1)
    lanes = (lane == 0, lane == width - 1)
    level = group * SUB + lax.broadcasted_iota(jnp.int32, (SUB, width), 0)

    def halo_row(row):
        return REACH + row if row < 0 else row - rows

    def depth_row(row):
        if 0 <= row < rows:
            line = depth_ref[row : row + 1, :]
        else:
            at = halo_row(row) * height + base + 6
            line = halo_top[at : at + 1, :].astype(jnp.int32)
        return jnp.broadcast_to(line, (SUB, width))

    def speed_row(which, row):
        if 0 <= row < rows:
            return uv_ref[which, pl.ds(row, SUB, stride=rows), :]
        if row < 0:
            at = base + (3 + row if which == 0 else 5 + row)
        else:
            at = base + 3 * which + row - rows
        return halo_ref[pl.ds(at, SUB, stride=height), :]

    here = depth_row(low - 3)
    for row in range(low - 3, high + 2):
        above = depth_row(row + 1)
        at = row - (low - 3)
        open_east = level < jnp.minimum(here, above)
        east[at] = jnp.where(open_east, sub_step * speed_row(0, row), 0.0)
        if row >= low - 2:
            beyond = jnp.where(lanes[1], 0, pltpu.roll(here, width - 1, 1))
            open_north = level < jnp.minimum(here, beyond)
            north[at] = jnp.where(open_north, sub_step * speed_row(1, row), 0.0)
        here = above

    for row in range(tall):
        shade[row] = jnp.zeros((SUB, width), jnp.float32)

    def one(t):
        def cell(row):
            if 0 <= row < rows:
                return c_ref[t + plan["skip"], pl.ds(row, SUB, stride=rows), :]
            at = REACH * (t + first) + halo_row(row)
            return halo_ref[pl.ds(at, SUB, stride=height), :]

        kept = {}

        def cells(row):
            if row not in kept:
                kept[row] = cell(row)
            return kept[row]

        def east_speed(row):
            return east[row - (low - 3)]

        def north_speed(row):
            return north[row - (low - 3)]

        before = Rows(cells, east_speed, north_speed, lanes)
        return Rows(before.new, east_speed, north_speed, lanes)

    unroll = plan["unroll"]

    def some(index, _):
        numbers = [index * unroll + k for k in range(unroll)]
        streams = [one(t) for t in numbers]
        factors = [attenuation[me * tracers_here + first + t] for t in numbers]
        for row in range(low, high):
            total = shade[row - low]
            for t, stream, factor in zip(numbers, streams, factors):
                value = stream.new(row)
                total = total + factor * jnp.abs(value)
                start = t * tall + row - low
                if shared > 1:
                    for part in range(shared):
                        slot = lax.bitwise_xor(me, group * shared + part)
                        buffer[slot, pl.ds(start, own, stride=count * tall), :] = value[
                            part * own : (part + 1) * own
                        ]
                else:
                    start = start + lax.rem(step, pieces) * SUB * count * tall
                    buffer[step // pieces, pl.ds(start, SUB, stride=count * tall), :] = value
            shade[row - low] = total
        return 0

    lax.fori_loop(0, count // unroll, some, 0)

    for part in range(shared):
        dest = group * shared + part if shared > 1 else group // pieces
        for row in range(tall):
            value = shade[row][part * min(own, SUB) : (part + 1) * min(own, SUB)]
            line = jnp.sum(value, axis=0, keepdims=True)
            if pieces > 1:
                old = jnp.where(lax.rem(step, pieces) == 0, 0.0, sums[dest, row : row + 1, :])
                line = line + old
            sums[dest, row : row + 1, :] = line

    def copy(slot, start, size, which):
        at = pl.ds(start, size)
        return pltpu.make_async_copy(
            buffer.at[slot, at, :], outs[slot].at[at, :], sems.at[slot, which]
        )

    for slot in range(devices):

        @pl.when(step == (slot // shared) * pieces + pieces - 1)
        def _():
            copy(slot, 0, main, 0).start()

    @pl.when(step == levels // SUB - 1)
    def _():
        for slot in range(devices):
            dest = lax.bitwise_xor(me, slot)
            above = jnp.zeros((tall, width), jnp.float32)
            for other in range(devices):
                above = above + jnp.where(other < dest, sums[other], 0.0)
            buffer[slot, main : main + tall, :] = above
        for slot in range(devices):
            copy(slot, main, tall, 1).start()
        for slot in range(devices):
            copy(slot, 0, main, 0).wait()
            copy(slot, main, tall, 1).wait()


def advect(species, currents, depth, attenuation, me, devices, first, count, low, high, halo, name):
    tracers, levels, rows, width = species.shape
    own = levels // devices
    shared, pieces = max(1, SUB // own), max(1, own // SUB)
    tall = high - low
    total = (own * count + 1) * tall
    height = REACH * tracers + EXTRA
    block = count if first % count == 0 else tracers
    plan = dict(
        rows=rows,
        levels=levels,
        tracers=tracers,
        first=first,
        count=count,
        own_levels=own,
        low=low,
        high=high,
        width=width,
        halo=halo is not None,
        skip=0 if block == count else first,
        unroll=2 if count % 2 == 0 else 1,
    )

    def group(step, me_ref):
        if shared > 1:
            return lax.bitwise_xor(me_ref[0] // shared, step)
        return lax.bitwise_xor(me_ref[0], step // pieces) * pieces + lax.rem(step, pieces)

    in_specs = [
        pl.BlockSpec(memory_space=pltpu.SMEM),
        pl.BlockSpec(
            (block, SUB * rows, width),
            lambda q, m: (first // count if block == count else 0, group(q, m), 0),
        ),
        pl.BlockSpec((2, SUB * rows, width), lambda q, m: (0, group(q, m), 0)),
        pl.BlockSpec((rows, width), lambda q, m: (0, 0)),
    ]
    args = [
        me,
        attenuation,
        species.reshape(tracers, levels * rows, width),
        currents.reshape(2, levels * rows, width),
        depth,
    ]
    if halo is not None:
        flat = halo.reshape(levels * height, width)
        in_specs += [
            pl.BlockSpec((SUB * height, width), lambda q, m: (group(q, m), 0)),
            pl.BlockSpec((SUB * height, width), lambda q, m: (0, 0)),
        ]
        args += [flat, flat]
    area = tall * width * levels * count
    return pl.pallas_call(
        functools.partial(advect_kernel, plan),
        grid_spec=pltpu.PrefetchScalarGridSpec(
            num_scalar_prefetch=1,
            grid=(levels // SUB,),
            in_specs=in_specs,
            out_specs=[pl.BlockSpec(memory_space=pl.ANY)] * devices,
            scratch_shapes=[
                pltpu.VMEM((devices, total, width), jnp.float32),
                pltpu.VMEM((tall + 5, SUB, width), jnp.float32),
                pltpu.VMEM((tall + 5, SUB, width), jnp.float32),
                pltpu.VMEM((tall, SUB, width), jnp.float32),
                pltpu.VMEM((devices, tall, width), jnp.float32),
                pltpu.SemaphoreType.DMA((devices, 2)),
            ],
        ),
        out_shape=[jax.ShapeDtypeStruct((total, width), jnp.float32)] * devices,
        name=name,
        cost_estimate=pl.CostEstimate(
            flops=area * 60, transcendentals=0, bytes_accessed=area * 16
        ),
    )(*args)


def react_kernel(plan, me_ref, consumed, attenuation, speeds, *refs):
    counts, tracers_here, own, devices, block, tall, width, levels = (
        plan["counts"],
        plan["tracers"],
        plan["own_levels"],
        plan["devices"],
        plan["block"],
        plan["tall"],
        plan["width"],
        plan["levels"],
    )
    parts = len(counts)
    data = [refs[p * devices : (p + 1) * devices] for p in range(parts)]
    refs = refs[parts * devices :]
    planes = refs[: parts * devices]
    refs = refs[parts * devices :]
    sun, depth, heat = refs[:3]
    out, heat_out, above, gain, share, inverse = refs[3 + plan["aliased"] :]
    me = me_ref[0]
    first_level = me * own + pl.program_id(0) * block
    band = pl.program_id(1)
    at = pl.ds(pl.multiple_of(band * SUB, SUB), SUB)
    layer = column_optical / levels

    @pl.when((pl.program_id(0) == 0) & (band == 0))
    def _():
        total = planes[0][...]
        for plane in planes[1:]:
            total = total + plane[...]
        above[...] = (total + (me * own).astype(jnp.float32) * water_clear) * layer

        def fill(t, _):
            inverse[consumed[t]] = t
            return 0

        lax.fori_loop(0, devices * tracers_here, fill, 0)

    pieces = []
    first = 0
    for p, count in enumerate(counts):
        pieces += [(p, slot, t, first + t) for slot in range(devices) for t in range(count)]
        first += count

    def one(level, _):
        def load(p, slot, t):
            offset = (level * counts[p] + t) * tall + band * SUB
            return data[p][slot][pl.ds(pl.multiple_of(offset, SUB), SUB), :]

        total = jnp.zeros((SUB, width), jnp.float32)
        for p, slot, t, local in pieces:
            number = lax.bitwise_xor(me, slot) * tracers_here + local
            value = load(p, slot, t)
            size = jnp.abs(value)
            total = total + attenuation[number] * size
            share[number] = value / (nutrient_half + size)
            gain[number] = speeds[number] * value
        optical = (water_clear + total) * layer
        overhead = above[at, :]
        above[at, :] = overhead + optical
        caught = sun[...] * jnp.exp(-overhead) * (1.0 - jnp.exp(-optical))
        mean_light = caught / optical
        wet = jnp.where(first_level + level < depth[...], 1.0, 0.0)
        light = wet * (mean_light / (mean_light + light_half))
        heat_out[level] = wet * (heat[level] + warming_coefficient * (caught * wet))
        for p, slot, t, local in pieces:
            number = lax.bitwise_xor(me, slot) * tracers_here + local
            taken = gain[number] * share[consumed[number]]
            lost = gain[inverse[number]] * share[number]
            out[number, level] = load(p, slot, t) + light * (taken - lost)
        return 0

    lax.fori_loop(0, block, one, 0)


def react(parts, counts, me, consumed, attenuation, speeds, sun, depth, heat, old, low, high, block, levels, name):
    devices = len(parts[0])
    rows, width = sun.shape
    own = heat.shape[0]
    tracers_here = sum(counts)
    every = devices * tracers_here
    tall = high - low
    place = low // SUB
    plan = dict(
        counts=counts,
        tracers=tracers_here,
        own_levels=own,
        devices=devices,
        block=block,
        tall=tall,
        width=width,
        levels=levels,
        aliased=0 if old is None else 2,
    )
    smem = pl.BlockSpec(memory_space=pltpu.SMEM)
    in_specs = [smem, smem, smem]
    args = [me, consumed, attenuation, speeds]
    for part, count in zip(parts, counts):
        in_specs += [pl.BlockSpec((block * count * tall, width), lambda q, r, m: (q, 0))] * devices
        args += part
    for part, count in zip(parts, counts):
        in_specs += [pl.BlockSpec((tall, width), lambda q, r, m, at=own * count: (at, 0))] * devices
        args += part
    band = pl.BlockSpec((SUB, width), lambda q, r, m: (place + r, 0))
    heat_spec = pl.BlockSpec((block, SUB, width), lambda q, r, m: (q, place + r, 0))
    in_specs += [band, band, heat_spec]
    args += [sun, depth, heat]
    aliases = {}
    if old is not None:
        aliases = {len(args): 0, len(args) + 1: 1}
        in_specs += [pl.BlockSpec(memory_space=pl.ANY)] * 2
        args += list(old)
    area = tall * width * own * every
    return pl.pallas_call(
        functools.partial(react_kernel, plan),
        grid_spec=pltpu.PrefetchScalarGridSpec(
            num_scalar_prefetch=1,
            grid=(own // block, tall // SUB),
            in_specs=in_specs,
            out_specs=[
                pl.BlockSpec((every, block, SUB, width), lambda q, r, m: (0, q, place + r, 0)),
                heat_spec,
            ],
            scratch_shapes=[
                pltpu.VMEM((tall, width), jnp.float32),
                pltpu.VMEM((every, SUB, width), jnp.float32),
                pltpu.VMEM((every, SUB, width), jnp.float32),
                pltpu.SMEM((every,), jnp.int32),
            ],
        ),
        out_shape=[
            jax.ShapeDtypeStruct((every, own, rows, width), jnp.float32),
            jax.ShapeDtypeStruct(heat.shape, jnp.float32),
        ],
        input_output_aliases=aliases,
        name=name,
        cost_estimate=pl.CostEstimate(flops=area * 20, transcendentals=0, bytes_accessed=area * 8),
    )(*args)


def exchange(blocks, axis):
    devices = len(blocks)
    got = {0: blocks[0]}
    for offset in sorted(range(1, devices), reverse=True):
        pairs = [(i, i ^ offset) for i in range(devices)]
        got[offset] = lax.ppermute(blocks[offset], axis, pairs)
    return [got[k] for k in range(devices)]


def on_device(
    species,
    currents,
    heat,
    depth,
    consumed,
    attenuation,
    speeds,
    sun,
):
    devices = lax.axis_size("tracer")
    tiles = lax.axis_size("tile")
    tracers, levels, rows, width = species.shape
    own = heat.shape[0]
    place = lax.axis_index("tracer")
    me = place.astype(jnp.int32).reshape(1)
    forward = [(i, (i + 1) % tiles) for i in range(tiles)]
    backward = [(target, source) for source, target in forward]
    edge = SUB
    half = tracers // 2
    base = REACH * tracers

    send = functools.partial(advect, species, currents, depth, attenuation, me, devices)
    inner_a = exchange(send(0, half, edge, rows - edge, None, "inner_a"), "tracer")
    to_next, to_previous = pack(species, currents, heat, depth)
    from_previous = lax.ppermute(to_next, "tile", forward)
    from_next = lax.ppermute(to_previous, "tile", backward)
    inner_b = exchange(send(half, tracers - half, edge, rows - edge, None, "inner_b"), "tracer")
    top = exchange(send(0, tracers, 0, edge, from_previous, "top"), "tracer")
    bottom = exchange(send(0, tracers, rows - edge, rows, from_next, "bottom"), "tracer")

    first_level = place * own
    below = lax.dynamic_slice_in_dim(from_previous, first_level, own, 0)
    above = lax.dynamic_slice_in_dim(from_next, first_level, own, 0)
    flow = lax.dynamic_slice_in_dim(currents, first_level, own, 1)
    flow_one = jnp.stack(
        [
            jnp.concatenate(
                [below[:, base + 2 : base + 3], flow[0], above[:, base : base + 1]], axis=1
            ),
            jnp.concatenate(
                [below[:, base + 4 : base + 5], flow[1], above[:, base + 3 : base + 4]], axis=1
            ),
        ]
    )
    heat_one = jnp.concatenate(
        [
            from_previous[:own, base + 5 : base + 6],
            heat,
            from_next[:own, base + 5 : base + 6],
        ],
        axis=1,
    )
    depth_one = jnp.concatenate(
        [
            from_previous[REACH - 1 : REACH, base + 6].astype(jnp.int32),
            depth,
            from_next[0:1, base + 6].astype(jnp.int32),
        ],
        axis=0,
    )
    level_numbers = first_level + jnp.arange(own, dtype=jnp.int32)
    wet_one = (level_numbers[:, None, None] < depth_one[None]).astype(jnp.float32)
    velocity, heat_curve = velocity_advance(flow_one, wet_one, heat_one)
    calm = heat + step_duration * spreading_coefficient * heat_curve

    def finish(parts, counts, old, low, high, block, name):
        return react(
            parts,
            counts,
            me,
            consumed,
            attenuation,
            speeds,
            sun,
            depth,
            calm,
            old,
            low,
            high,
            block,
            levels,
            name,
        )

    block = max(1, own // 2)
    done = finish(
        [inner_a, inner_b], [half, tracers - half], None, edge, rows - edge, block, "react_inner"
    )
    done = finish([top], [tracers], done, 0, edge, block, "react_top")
    done = finish([bottom], [tracers], done, rows - edge, rows, block, "react_bottom")
    return done[0], velocity, done[1]


def solution(mesh):
    return jax.shard_map(
        on_device,
        mesh=mesh,
        in_specs=(
            P(("groups", "tracer"), None, "tile", None),
            P(None, "groups", "tile", None),
            P(("groups", "tracer"), "tile", None),
            P(("groups", "tile"), None),
            P(),
            P(),
            P(),
            P(("groups", "tile"), None),
        ),
        out_specs=(
            P("groups", "tracer", "tile", None),
            P(None, ("groups", "tracer"), "tile", None),
            P(("groups", "tracer"), "tile", None),
        ),
        check_vma=False,
    )
```
